32 devices in a mesh: tok: 8 (over z, core), par: 4 (over y, x).
Axes of the slice: x: 2, y: 2, z: 4, core: 2. Of those that a mesh axis runs over, the one named last changes fastest.
Arguments:
- query_grads: bfloat16 [4, 8192, 28672], P(None, 'tok', 'par'), as said below
- start_block: bfloat16 [28672, 128], P('par', 'tok'), may hold values from -6 to 6
- hooked_out: bfloat16 [2048, 8192], P('tok', 'par'), may hold values from -6 to 6
- hooked_in: bfloat16 [2048, 28672], P('tok', 'par'), may hold values from -6 to 6
Outputs:
- scores: float32 [4, 2048], P(None, 'tok')
The draws below stay inside these ranges and needn't reach their ends.
Inputs may be any that keep to these rules, and one draw needn't show every extreme that they name: `query_grads`: Real-valued gradient matrices, of full rank.
All inputs are finite; a program needn't handle non-finite values.
Results may differ from the reference program's by a relative error of at most 0.006.
Values may be sent and summed in bfloat16 or wider, within the bound.
No kernel may reach another device: no remote copies, remote signals or barrier semaphores. Data moves between devices by JAX's collectives and lax.ppermute only.
A program may use at most 128 MiB of HBM per device.

```python
import math
import jax
import jax.numpy as jnp
from jax import lax

DOUT = 8192
DIN = 28672
QUERIES = 4
RANK = 32
ITERS = 2
TOKENS = 2048


def draw_query_grads(key, part):
    key_base, key_rows, key_cols = jax.random.split(key, 3)
    base = jnp.clip(jax.random.normal(key_base, (QUERIES, DOUT, DIN), jnp.float32), -6.0, 6.0)
    row_scale = jnp.exp(jax.random.uniform(key_rows, (QUERIES, DOUT, 1), jnp.float32, 0.0, math.log(10.0)))
    col_scale = jnp.exp(jax.random.uniform(key_cols, (QUERIES, 1, DIN), jnp.float32, 0.0, math.log(10.0)))
    factor = 1.0 / (21.5 * math.sqrt(80.0 * DIN))
    return (base * row_scale * col_scale * factor).astype(jnp.bfloat16)


def block_levels(stream_key, shape, cuts, low, high):
    gain, own = 1.0, jax.random.fold_in(stream_key, 6)
    for dim, blocks in cuts:
        steps = jnp.exp(jax.random.uniform(jax.random.fold_in(own, dim), (blocks,), jnp.float32, low / len(cuts), high / len(cuts)))
        gain = gain * jnp.repeat(steps, shape[dim] // blocks).reshape([-1 if axis == dim else 1 for axis in range(len(shape))])
    return gain


def centred(key, shape, deviation, most, cuts=(), kind=jnp.bfloat16):
    level = block_levels(key, shape, cuts, -0.22, 0.18) if cuts else 1.0
    result = jax.random.normal(key, shape, jnp.float32) * deviation * level
    return jnp.minimum(jnp.maximum(result, -most), most).astype(kind)


def setup_inputs(seed: int = 0) -> dict:
    keys = jax.random.split(jax.random.key(seed), 5)
    query_grads = draw_query_grads(jax.random.fold_in(keys[4], 71), 0)
    start_block = centred(keys[1], (DIN, QUERIES * RANK), 1.0, 6.0, ((0, 4), (1, 8)))
    hooked_out = centred(keys[2], (TOKENS, DOUT), 1.0, 6.0, ((0, 8), (1, 4)))
    hooked_in = centred(keys[3], (TOKENS, DIN), 1.0, 6.0, ((0, 8), (1, 4)))
    return {"query_grads": query_grads, "start_block": start_block, "hooked_out": hooked_out, "hooked_in": hooked_in}


def local_gram(images):
    blocks = images.reshape(images.shape[0], QUERIES, RANK)
    return jnp.einsum('oqr,oqs->qrs', blocks, blocks, precision=lax.Precision.HIGHEST)

def from_gram(images, gram_sum):
    blocks = images.reshape(images.shape[0], QUERIES, RANK)
    chol_factor = jnp.linalg.cholesky(gram_sum)
    solved = lax.linalg.triangular_solve(chol_factor, jnp.transpose(blocks, (1, 2, 0)), left_side=True, lower=True)
    return jnp.transpose(solved, (2, 0, 1)).reshape(images.shape).astype(jnp.bfloat16)

def reference(query_grads, start_block, hooked_out, hooked_in):
    subspace = start_block
    full_basis = None
    for iteration in range(ITERS):
        pieces = []
        for query in range(QUERIES):
            cols = subspace[:, query * RANK:(query + 1) * RANK]
            pieces.append(jnp.dot(query_grads[query].astype(jnp.float32), cols.astype(jnp.float32), preferred_element_type=jnp.float32))
        images = jnp.concatenate(pieces, axis=1)
        full_basis = from_gram(images, local_gram(images))
        backs = []
        for query in range(QUERIES):
            cols = full_basis[:, query * RANK:(query + 1) * RANK]
            backs.append(jnp.dot(cols.T.astype(jnp.float32), query_grads[query].astype(jnp.float32), preferred_element_type=jnp.float32).T)
        subspace = jnp.concatenate(backs, axis=1).astype(jnp.bfloat16)
    out_proj = jnp.dot(hooked_out.astype(jnp.float32), full_basis.astype(jnp.float32), preferred_element_type=jnp.float32)
    in_proj = jnp.dot(hooked_in.astype(jnp.float32), subspace.astype(jnp.float32), preferred_element_type=jnp.float32)
    scores = (out_proj * in_proj).reshape(out_proj.shape[0], QUERIES, RANK).sum(axis=2)
    return scores.T
```

```python
import functools
import jax
import jax.numpy as jnp
from jax import lax
from jax.experimental import pallas as pl
from jax.experimental.pallas import tpu as pltpu
from jax.sharding import PartitionSpec as P

RANK = 32
ITERS = 2
CORES = 2
F32, BF16 = jnp.float32, jnp.bfloat16
HIGH = lax.Precision.HIGHEST
NT = (((1,), (1,)), ((), ()))
ANY = pl.BlockSpec(memory_space=pl.ANY)
VMEM = pl.BlockSpec(memory_space=pltpu.VMEM)
SMEM = pl.BlockSpec(memory_space=pltpu.SMEM)
VMEM_BYTES = 60 * 1024 * 1024


def params():
    return pltpu.CompilerParams(vmem_limit_bytes=VMEM_BYTES)


def cost(flops, nbytes):
    return pl.CostEstimate(flops=int(flops), bytes_accessed=int(nbytes), transcendentals=0)


ROW_CHUNKS = 8


def images_body(where, mine_ref, other_ref, grads_ref, *rest, slot, aliased):
    out_ref, buf, sems = rest[1:] if aliased else rest
    query, core = where[0], where[1]
    rows = buf.shape[1]

    def fetch(i):
        return pltpu.make_async_copy(
            grads_ref.at[query, pl.ds(i * rows, rows), :], buf.at[i], sems.at[i]
        )

    for i in range(ROW_CHUNKS):
        fetch(i).start()
    mine, other = mine_ref[...], other_ref[...]
    vectors = jnp.concatenate(
        [jnp.where(core == 0, mine, other), jnp.where(core == 0, other, mine)], axis=0
    )

    def body(i, carry):
        fetch(i).wait()
        out_ref[0, :, pl.ds(pl.multiple_of(i * rows, 128), rows)] = lax.dot_general(
            vectors, buf[i], NT, preferred_element_type=F32
        )
        return carry

    lax.fori_loop(0, ROW_CHUNKS, body, 0)


def images_of_query(where, mine, other, grads, slot, slots, earlier=None):
    _, rows, cols = grads.shape
    aliased = earlier is not None
    return pl.pallas_call(
        functools.partial(images_body, slot=slot, aliased=aliased),
        grid=(1,),
        in_specs=[SMEM, VMEM, VMEM, ANY] + ([ANY] if aliased else []),
        out_specs=pl.BlockSpec((1, RANK, rows), lambda i: (slot, 0, 0)),
        out_shape=jax.ShapeDtypeStruct((slots, RANK, rows), F32),
        scratch_shapes=[
            pltpu.VMEM((ROW_CHUNKS, rows // ROW_CHUNKS, cols), BF16),
            pltpu.SemaphoreType.DMA((ROW_CHUNKS,)),
        ],
        input_output_aliases={4: 0} if aliased else {},
        cost_estimate=cost(2 * RANK * rows * cols * 8, 2 * rows * cols),
        compiler_params=params(),
    )(where, mine, other, grads, *([earlier] if aliased else []))


SLOTS = 8


def back_body(where, basis_ref, grads_ref, mine_ref, other_ref, buf, sems, *, first, width):
    core = where[1]
    queries, half, cols = mine_ref.shape
    steps = queries * (cols // width)

    def fetch(step):
        query, block = lax.rem(step, queries), lax.div(step, queries)
        slot = lax.rem(step, SLOTS)
        start = pl.multiple_of(first + block * width, 128)
        return pltpu.make_async_copy(
            grads_ref.at[query, :, pl.ds(start, width)], buf.at[slot], sems.at[slot]
        )

    for step in range(min(SLOTS - 1, steps)):
        fetch(jnp.int32(step)).start()

    def body(step, carry):
        @pl.when(step + SLOTS - 1 < steps)
        def _():
            fetch(step + SLOTS - 1).start()

        query, block = lax.rem(step, queries), lax.div(step, queries)
        fetch(step).wait()
        product = jnp.dot(
            basis_ref[query], buf[lax.rem(step, SLOTS)], preferred_element_type=F32
        )
        low, high = product[:half], product[half:]
        where_to = pl.ds(pl.multiple_of(block * width, 128), width)
        mine_ref[query, :, where_to] = jnp.where(core == 0, low, high)
        other_ref[query, :, where_to] = jnp.where(core == 0, high, low).astype(BF16)
        return carry

    lax.fori_loop(0, steps, body, 0)


def back_project(where, basis, grads, first, cols, width):
    queries, rows, _ = grads.shape
    half = RANK // CORES
    return pl.pallas_call(
        functools.partial(back_body, first=first, width=width),
        in_specs=[SMEM, VMEM, ANY],
        out_specs=[VMEM, VMEM],
        out_shape=[
            jax.ShapeDtypeStruct((queries, half, cols), F32),
            jax.ShapeDtypeStruct((queries, half, cols), BF16),
        ],
        scratch_shapes=[
            pltpu.VMEM((SLOTS, rows, width), BF16),
            pltpu.SemaphoreType.DMA((SLOTS,)),
        ],
        cost_estimate=cost(2 * RANK * queries * rows * cols * 8, 2 * queries * rows * cols),
        compiler_params=params(),
    )(where, basis, grads)


def gram_body(where, *refs):
    pairs, (images_ref, gram_ref) = refs[:-2], refs[-2:]
    chip = where[0]
    queries = images_ref.shape[0]
    slot = 0
    for held, received in zip(pairs[0::2], pairs[1::2]):
        for i in range(held.shape[0]):
            images_ref[chip ^ slot] = held[i] + received[i]
            slot += 1
    for query in range(queries):
        block = images_ref[query]
        gram_ref[:, query * RANK : (query + 1) * RANK] = lax.dot_general(
            block, block, NT, precision=HIGH, preferred_element_type=F32
        )


def local_gram(where, pairs):
    flat = [part for pair in pairs for part in pair]
    queries = sum(held.shape[0] for held, _ in pairs)
    rows = flat[0].shape[2]
    return pl.pallas_call(
        gram_body,
        in_specs=[SMEM] + [VMEM] * len(flat),
        out_specs=[VMEM, VMEM],
        out_shape=[
            jax.ShapeDtypeStruct((queries, RANK, rows), F32),
            jax.ShapeDtypeStruct((RANK, queries * RANK), F32),
        ],
        cost_estimate=cost(12 * RANK * RANK * queries * rows, 16 * queries * RANK * rows),
        compiler_params=params(),
    )(where, *flat)


def basis_body(gram_ref, received_ref, images_ref, basis_ref):
    queries = images_ref.shape[0]
    total = queries * RANK
    gram = gram_ref[...] + received_ref[...]
    stacked = jnp.concatenate(
        [gram[:, q * RANK : (q + 1) * RANK] for q in range(queries)], axis=0
    )
    row = lax.broadcasted_iota(jnp.int32, (total, RANK), 0) % RANK
    col = lax.broadcasted_iota(jnp.int32, (total, RANK), 1)
    table = jnp.concatenate([stacked, jnp.where(row == col, 1.0, 0.0).astype(F32)], axis=1)
    row = lax.broadcasted_iota(jnp.int32, (total, 2 * RANK), 0) % RANK
    table = table.reshape(queries, RANK, 2 * RANK)
    row = row.reshape(queries, RANK, 2 * RANK)
    scales = jnp.zeros((queries, RANK, 1), F32)
    for k in range(RANK):
        pivot_row = table[:, k : k + 1, :]
        pivot = pivot_row[:, :, k : k + 1]
        factor = table[:, :, k : k + 1] / pivot
        scales = jnp.where(row[:, :, :1] == k, lax.rsqrt(pivot), scales)
        table = table - jnp.where(row > k, factor * pivot_row, 0.0)
    inverse = table[:, :, RANK:] * scales
    for q in range(queries):
        basis_ref[q] = jnp.dot(
            inverse[q], images_ref[q], precision=HIGH, preferred_element_type=F32
        ).astype(BF16)


def orthonormal(gram, received, images):
    return pl.pallas_call(
        basis_body,
        in_specs=[VMEM] * 3,
        out_specs=VMEM,
        out_shape=jax.ShapeDtypeStruct(images.shape, BF16),
        cost_estimate=cost(12 * RANK * images.size + 10**9, 6 * images.size),
        compiler_params=params(),
    )(gram, received, images)


def combine_body(where, mine_ref, received_ref, own_ref, *send_refs):
    chip = where[0]
    own_ref[...] = mine_ref[chip] + received_ref[chip].astype(F32)
    for d, send_ref in enumerate(send_refs, 1):
        send_ref[...] = (mine_ref[chip ^ d] + received_ref[chip ^ d].astype(F32)).astype(BF16)


def combine(where, mine, received):
    chips, half, cols = mine.shape
    return pl.pallas_call(
        combine_body,
        in_specs=[SMEM, VMEM, VMEM],
        out_specs=[VMEM] * chips,
        out_shape=[jax.ShapeDtypeStruct((half, cols), F32)]
        + [jax.ShapeDtypeStruct((half, cols), BF16)] * (chips - 1),
        cost_estimate=cost(mine.size, 10 * mine.size),
        compiler_params=params(),
    )(where, mine, received)


def xor_permute(x, axis, size, bits):
    return lax.ppermute(x, axis, [(i, i ^ bits) for i in range(size)])


def fast(query_grads, start_block, hooked_out, hooked_in, *, toks, pars):
    queries, rows, cols = query_grads.shape
    chips = toks // CORES
    tok, par = lax.axis_index("tok"), lax.axis_index("par")
    chip, core = tok // CORES, tok % CORES
    where = [jnp.stack([chip ^ d, core]).astype(jnp.int32) for d in range(chips)]

    def tok_swap(x, bits):
        return xor_permute(x, "tok", toks, bits)

    def images_from(piece):
        pieces = [piece] + [tok_swap(piece, CORES * d) for d in range(1, chips)]
        held, parts = None, []
        for d in range(chips):
            other = tok_swap(pieces[d], 1)
            held = images_of_query(where[d], pieces[d], other, query_grads, d % 2, 2, held)
            if d % 2 == 1:
                parts.append(held)
                held = None
        bits = [1 << i for i in range(pars.bit_length() - 1)]
        pairs = []
        for i, part in enumerate(parts):
            order = bits if i % 2 == 0 else bits[::-1]
            for b in order[:-1]:
                part = part + xor_permute(part, "par", pars, b)
            pairs.append((part, xor_permute(part, "par", pars, order[-1])))
        return pairs

    def basis_from(pairs):
        images, gram = local_gram(where[0], pairs)
        bits = [1 << i for i in range(toks.bit_length() - 1)]
        for b in bits[:-1]:
            gram = gram + tok_swap(gram, b)
        return orthonormal(gram, tok_swap(gram, bits[-1]), images)

    def back_piece(basis):
        mine, other = back_project(where[0], basis, query_grads, 0, cols, cols // 8)
        received = tok_swap(other, 1)
        own, *sends = combine(where[0], mine, received)
        total = own
        for d, send in enumerate(sends, 1):
            total = total + tok_swap(send, CORES * d).astype(F32)
        return total.astype(BF16)

    piece = start_block.T
    basis = None
    for _ in range(ITERS):
        basis = basis_from(images_from(piece))
        piece = back_piece(basis)

    flat = basis.reshape(queries * RANK, rows)
    got = jnp.where(chip == par, flat, jnp.zeros_like(flat))
    for d in range(1, chips):
        sends = [
            ((p * CORES + c) * pars + p, ((p ^ d) * CORES + c) * pars + p)
            for p in range(pars)
            for c in range(CORES)
        ]
        got = got + lax.ppermute(flat, ("tok", "par"), sends)
    mate = tok_swap(got, 1)
    low, high = jnp.where(core == 0, got, mate), jnp.where(core == 0, mate, got)
    basis_par = jnp.concatenate([low, high], axis=1)
    out_proj = lax.dot_general(basis_par, hooked_out, NT, preferred_element_type=F32)

    half = RANK // CORES
    in_parts = []
    for d in range(chips):
        mine = piece if d == 0 else tok_swap(piece, CORES * d)
        mate = tok_swap(mine, 1)
        both = jnp.concatenate([jnp.where(core == 0, mine, mate), jnp.where(core == 0, mate, mine)])
        in_parts.append(lax.dot_general(both, hooked_in, NT, preferred_element_type=F32))
    in_rel = jnp.stack(in_parts)
    out_rel = out_proj.reshape(queries, RANK, -1)
    order = jnp.stack([chip ^ d for d in range(chips)])
    out_rel = jnp.stack([out_rel[chip ^ d] for d in range(chips)])
    whole = jnp.stack([out_rel, in_rel])
    for b in [1 << i for i in range(pars.bit_length() - 1)]:
        whole = whole + xor_permute(whole, "par", pars, b)
    rel = (whole[0] * whole[1]).sum(axis=1)
    return jnp.stack([rel[chip ^ q] for q in range(queries)])


def plain(query_grads, start_block, hooked_out, hooked_in):
    queries, rows_tok = query_grads.shape[:2]
    cols_par = hooked_out.shape[1]

    def blocked(x):
        return x.reshape(x.shape[0], queries, RANK)

    subspace = lax.all_gather(start_block, "tok", axis=1, tiled=True)
    basis = None
    for _ in range(ITERS):
        partial = jnp.einsum(
            "qoi,iqr->oqr", query_grads, blocked(subspace), preferred_element_type=F32
        )
        images = lax.psum(partial.reshape(rows_tok, queries * RANK), "par")
        blocks = blocked(images)
        gram = lax.psum(jnp.einsum("oqr,oqs->qrs", blocks, blocks, precision=HIGH), "tok")
        solved = lax.linalg.triangular_solve(
            jnp.linalg.cholesky(gram), jnp.transpose(blocks, (1, 2, 0)), left_side=True, lower=True
        )
        basis = jnp.transpose(solved, (2, 0, 1)).reshape(images.shape).astype(BF16)
        back = jnp.einsum(
            "qoi,oqr->iqr", query_grads, blocked(basis), preferred_element_type=F32
        )
        subspace = lax.psum(back.reshape(back.shape[0], queries * RANK), "tok").astype(BF16)
    gathered = lax.all_gather(basis, "tok", axis=0, tiled=True)
    basis_par = lax.dynamic_slice_in_dim(gathered, lax.axis_index("par") * cols_par, cols_par, 0)
    out_proj = jnp.dot(hooked_out, basis_par, preferred_element_type=F32)
    in_proj = jnp.dot(hooked_in, subspace, preferred_element_type=F32)
    whole_out, whole_in = lax.psum((out_proj, in_proj), "par")
    return (whole_out * whole_in).reshape(whole_out.shape[0], queries, RANK).sum(axis=2).T


def solution(mesh):
    toks, pars = mesh.shape["tok"], mesh.shape["par"]

    def on_device(query_grads, start_block, hooked_out, hooked_in):
        if toks == CORES * query_grads.shape[0] and toks == CORES * pars:
            run = functools.partial(fast, toks=toks, pars=pars)
        else:
            run = plain
        return run(query_grads, start_block, hooked_out, hooked_in)

    placed = (P(None, "tok", "par"), P("par", "tok"), P("tok", "par"), P("tok", "par"))
    return jax.shard_map(
        on_device, mesh=mesh, in_specs=placed, out_specs=P(None, "tok"), check_vma=False
    )
```

```python
import functools
import jax
import jax.numpy as jnp
from jax import lax
from jax.experimental import pallas as pl
from jax.experimental.pallas import tpu as pltpu
from jax.sharding import PartitionSpec as P

RANK = 32
ITERS = 2
CORES = 2
F32, BF16 = jnp.float32, jnp.bfloat16
HIGH = lax.Precision.HIGHEST
NT = (((1,), (1,)), ((), ()))
ANY = pl.BlockSpec(memory_space=pl.ANY)
VMEM = pl.BlockSpec(memory_space=pltpu.VMEM)
SMEM = pl.BlockSpec(memory_space=pltpu.SMEM)
MIB = 1024 * 1024


def params(mebibytes=4):
    return pltpu.CompilerParams(vmem_limit_bytes=mebibytes * MIB)


def cost(flops, nbytes):
    return pl.CostEstimate(flops=int(flops), bytes_accessed=int(nbytes), transcendentals=0)


ROW_CHUNKS = 4
COL_CHUNKS = 8
STREAM_BANDS = 2
STREAM_COLS = 4
STREAMED = 1


def images_body(where, mine_ref, other_ref, grads_ref, *rest, mode, aliased, offset):
    out_ref, *rest = rest[1:] if aliased else rest
    query, core = where[0] ^ offset, where[1]
    rows = out_ref.shape[2] // ROW_CHUNKS

    def band(i):
        return pl.ds(pl.multiple_of(i * rows, 128), rows)

    def view(i):
        if mode == "stream":
            return rest[0].at[lax.rem(i, STREAM_BANDS)]
        return (grads_ref if mode == "held" else rest[0]).at[band(i), :]

    def fetch(i):
        return pltpu.make_async_copy(grads_ref.at[query, band(i), :], view(i), rest[1].at[i])

    if mode != "held":
        for i in range(STREAM_BANDS if mode == "stream" else ROW_CHUNKS):
            fetch(i).start()
    mine, other = mine_ref[...], other_ref[...]
    vectors = jnp.concatenate(
        [jnp.where(core == 0, mine, other), jnp.where(core == 0, other, mine)], axis=0
    )

    def body(i, carry):
        if mode != "held":
            fetch(i).wait()
        out_ref[0, :, band(i)] = lax.dot_general(
            vectors, view(i)[...], NT, preferred_element_type=F32
        )
        if mode == "stream":

            @pl.when(i + STREAM_BANDS < ROW_CHUNKS)
            def _():
                fetch(i + STREAM_BANDS).start()

        return carry

    lax.fori_loop(0, ROW_CHUNKS, body, 0)


def images_of_query(where, offset, mine, other, grads, mode, slot, slots, earlier=None):
    rows, cols = grads.shape[-2:]
    aliased, load = earlier is not None, mode == "load"
    scratch = []
    if mode == "stream":
        scratch.append(pltpu.VMEM((STREAM_BANDS, rows // ROW_CHUNKS, cols), BF16))
    if mode != "held":
        scratch.append(pltpu.SemaphoreType.DMA((ROW_CHUNKS,)))
    return pl.pallas_call(
        functools.partial(images_body, mode=mode, aliased=aliased, offset=offset),
        grid=(1,),
        in_specs=[SMEM, VMEM, VMEM, VMEM if mode == "held" else ANY] + [ANY] * aliased,
        out_specs=[pl.BlockSpec((1, RANK, rows), lambda i: (slot, 0, 0))] + [VMEM] * load,
        out_shape=[jax.ShapeDtypeStruct((slots, RANK, rows), F32)]
        + [pltpu.VMEM((rows, cols), BF16)] * load,
        scratch_shapes=scratch,
        input_output_aliases={4: 0} if aliased else {},
        cost_estimate=cost(2 * RANK * rows * cols * 8, 2 * rows * cols),
        compiler_params=params(12 if mode == "stream" else 3),
    )(where, mine, other, grads, *([earlier] if aliased else []))


def back_body(where, basis_ref, grads_ref, *rest, stream, ties, offset):
    mine_ref, other_ref, *rest = rest[ties:]
    query, core = where[0] ^ offset, where[1]
    half = mine_ref.shape[0]
    width = mine_ref.shape[1] // COL_CHUNKS
    vectors = basis_ref[query]

    def band(i):
        return pl.ds(pl.multiple_of(i * width, 128), width)

    def view(i):
        return rest[0].at[lax.rem(i, STREAM_COLS)] if stream else grads_ref.at[:, band(i)]

    def fetch(i):
        return pltpu.make_async_copy(grads_ref.at[query, :, band(i)], view(i), rest[1].at[i])

    if stream:
        for i in range(STREAM_COLS):
            fetch(i).start()

    def body(i, carry):
        if stream:
            fetch(i).wait()
        product = jnp.dot(vectors, view(i)[...], preferred_element_type=F32)
        low, high = product[:half], product[half:]
        mine_ref[:, band(i)] = jnp.where(core == 0, low, high)
        other_ref[:, band(i)] = jnp.where(core == 0, high, low).astype(BF16)
        if stream:

            @pl.when(i + STREAM_COLS < COL_CHUNKS)
            def _():
                fetch(i + STREAM_COLS).start()

        return carry

    lax.fori_loop(0, COL_CHUNKS, body, 0)


def back_of_query(where, offset, basis, grads, after):
    rows, cols = grads.shape[-2:]
    stream = grads.ndim == 3
    half = RANK // CORES
    scratch = [
        pltpu.VMEM((STREAM_COLS, rows, cols // COL_CHUNKS), BF16),
        pltpu.SemaphoreType.DMA((COL_CHUNKS,)),
    ]
    return pl.pallas_call(
        functools.partial(back_body, stream=stream, ties=len(after), offset=offset),
        in_specs=[SMEM, VMEM, ANY if stream else VMEM] + [ANY] * len(after),
        out_specs=[VMEM, VMEM],
        out_shape=[
            jax.ShapeDtypeStruct((half, cols), F32),
            jax.ShapeDtypeStruct((half, cols), BF16),
        ],
        scratch_shapes=scratch if stream else [],
        cost_estimate=cost(2 * RANK * rows * cols * 8, 2 * rows * cols),
        compiler_params=params(12 if stream else 3),
    )(where, basis, grads, *after)


def gram_body(where, *refs):
    pairs, (images_ref, gram_ref) = refs[:-2], refs[-2:]
    chip = where[0]
    queries = images_ref.shape[0]
    slot = 0
    for held, received in zip(pairs[0::2], pairs[1::2]):
        for i in range(held.shape[0]):
            images_ref[chip ^ slot] = held[i] + received[i]
            slot += 1
    for query in range(queries):
        block = images_ref[query]
        gram_ref[:, query * RANK : (query + 1) * RANK] = lax.dot_general(
            block, block, NT, precision=HIGH, preferred_element_type=F32
        )


def local_gram(where, pairs):
    flat = [part for pair in pairs for part in pair]
    queries = sum(held.shape[0] for held, _ in pairs)
    rows = flat[0].shape[2]
    return pl.pallas_call(
        gram_body,
        in_specs=[SMEM] + [VMEM] * len(flat),
        out_specs=[VMEM, VMEM],
        out_shape=[
            jax.ShapeDtypeStruct((queries, RANK, rows), F32),
            jax.ShapeDtypeStruct((RANK, queries * RANK), F32),
        ],
        cost_estimate=cost(12 * RANK * RANK * queries * rows, 16 * queries * RANK * rows),
        compiler_params=params(),
    )(where, *flat)


def basis_body(images_ref, *refs):
    gram_refs, basis_ref = refs[:-1], refs[-1]
    queries = images_ref.shape[0]
    total = queries * RANK
    gram = gram_refs[0][...]
    for ref in gram_refs[1:]:
        gram = gram + ref[...]
    stacked = jnp.concatenate(
        [gram[:, q * RANK : (q + 1) * RANK] for q in range(queries)], axis=0
    )
    row = lax.broadcasted_iota(jnp.int32, (total, RANK), 0) % RANK
    col = lax.broadcasted_iota(jnp.int32, (total, RANK), 1)
    table = jnp.concatenate([stacked, jnp.where(row == col, 1.0, 0.0).astype(F32)], axis=1)
    row = lax.broadcasted_iota(jnp.int32, (total, 2 * RANK), 0) % RANK
    table = table.reshape(queries, RANK, 2 * RANK)
    row = row.reshape(queries, RANK, 2 * RANK)
    scales = jnp.zeros((queries, RANK, 1), F32)
    for k in range(RANK):
        pivot_row = table[:, k : k + 1, :]
        pivot = pivot_row[:, :, k : k + 1]
        factor = table[:, :, k : k + 1] / pivot
        scales = jnp.where(row[:, :, :1] == k, lax.rsqrt(pivot), scales)
        table = table - jnp.where(row > k, factor * pivot_row, 0.0)
    inverse = table[:, :, RANK:] * scales
    for q in range(queries):
        basis_ref[q] = jnp.dot(
            inverse[q], images_ref[q], precision=HIGH, preferred_element_type=F32
        ).astype(BF16)


def orthonormal(images, grams):
    return pl.pallas_call(
        basis_body,
        in_specs=[VMEM] * (1 + len(grams)),
        out_specs=VMEM,
        out_shape=jax.ShapeDtypeStruct(images.shape, BF16),
        cost_estimate=cost(12 * RANK * images.size + 10**9, 6 * images.size),
        compiler_params=params(),
    )(images, *grams)


def choose_body(where, held_ref, received_ref, out_ref, *, owners):
    wanted = where[2]
    own = functools.reduce(jnp.logical_or, [where[0] == wanted ^ bits for bits in owners])
    out_ref[...] = jnp.where(own, held_ref[...], received_ref[...])


def choose(where, held, received, owners):
    return pl.pallas_call(
        functools.partial(choose_body, owners=owners),
        in_specs=[SMEM, VMEM, VMEM],
        out_specs=VMEM,
        out_shape=jax.ShapeDtypeStruct(held.shape, held.dtype),
        cost_estimate=cost(held.size, 6 * held.size),
        compiler_params=params(),
    )(where, held, received)


def both_cores(core, mine, other, axis):
    return jnp.concatenate(
        [jnp.where(core == 0, mine, other), jnp.where(core == 0, other, mine)], axis=axis
    )


def project_out_body(where, mine_ref, other_ref, hooked_ref, out_ref, scratch):
    vectors = both_cores(where[1], mine_ref[...], other_ref[...], 1)
    queries = scratch.shape[0]
    scratch[...] = lax.dot_general(
        vectors, hooked_ref[...], NT, preferred_element_type=F32
    ).reshape(scratch.shape)
    for d in range(queries):
        out_ref[d] = scratch[where[0] ^ d]


def project_out(where, mine, other, hooked):
    shape = (mine.shape[0] // RANK, RANK, hooked.shape[0])
    return pl.pallas_call(
        project_out_body,
        in_specs=[SMEM, VMEM, VMEM, VMEM],
        out_specs=VMEM,
        out_shape=jax.ShapeDtypeStruct(shape, F32),
        scratch_shapes=[pltpu.VMEM(shape, F32)],
        cost_estimate=cost(4 * mine.size * hooked.shape[0], 2 * hooked.size),
        compiler_params=params(),
    )(where, mine, other, hooked)


def project_in_body(where, mine_ref, other_ref, hooked_ref, *rest):
    vectors = both_cores(where[1], mine_ref[...], other_ref[...], 0)
    rest[-1][0] = lax.dot_general(vectors, hooked_ref[...], NT, preferred_element_type=F32)


def project_in(where, mine, other, hooked, slot, slots, earlier=None):
    tokens = hooked.shape[0]
    aliased = earlier is not None
    return pl.pallas_call(
        project_in_body,
        grid=(1,),
        in_specs=[SMEM, VMEM, VMEM, VMEM] + [ANY] * aliased,
        out_specs=pl.BlockSpec((1, RANK, tokens), lambda i: (slot, 0, 0)),
        out_shape=jax.ShapeDtypeStruct((slots, RANK, tokens), F32),
        input_output_aliases={4: 0} if aliased else {},
        cost_estimate=cost(4 * mine.size * tokens, 2 * hooked.size),
        compiler_params=params(),
    )(where, mine, other, hooked, *([earlier] if aliased else []))


def scores_body(where, *refs):
    sums, score_ref = [], refs[-1]
    for held_ref, received_ref in zip(refs[:-1:2], refs[1:-1:2]):
        sums += [held_ref[i] + received_ref[i] for i in range(held_ref.shape[0])]
    queries = len(sums) // 2
    for d in range(queries):
        score = (sums[d] * sums[queries + d]).sum(axis=0, keepdims=True)
        score_ref[pl.ds(where[0] ^ d, 1), :] = score


def token_scores(where, pairs):
    flat = [part for pair in pairs for part in pair]
    queries = sum(held.shape[0] for held, _ in pairs) // 2
    return pl.pallas_call(
        scores_body,
        in_specs=[SMEM] + [VMEM] * len(flat),
        out_specs=VMEM,
        out_shape=jax.ShapeDtypeStruct((queries, flat[0].shape[2]), F32),
        compiler_params=params(),
    )(where, *flat)


def xor_permute(x, axis, size, bits):
    return lax.ppermute(x, axis, [(i, i ^ bits) for i in range(size)])


def fast(query_grads, start_block, hooked_out, hooked_in, *, toks, pars):
    queries, rows, _ = query_grads.shape
    chips = toks // CORES
    tok, par = lax.axis_index("tok"), lax.axis_index("par")
    chip, core = tok // CORES, tok % CORES
    where = jnp.stack([chip, core, par]).astype(jnp.int32)
    par_bits = [1 << i for i in range(pars.bit_length() - 1)]
    held = [query_grads] * chips

    def tok_swap(x, bits):
        return xor_permute(x, "tok", toks, bits)

    def par_pair(x):
        for b in par_bits[:-1]:
            x = x + xor_permute(x, "par", pars, b)
        return x, xor_permute(x, "par", pars, par_bits[-1])

    def gathered(piece, step):
        pieces = [piece] + [tok_swap(piece, CORES * d) for d in range(1, chips)]
        for d in range(chips):
            other = tok_swap(pieces[d], 1)
            step(d, pieces[d], other)

    def images_from(piece):
        done = []

        def step(d, mine, other):
            earlier = done[-1] if d % 2 else None
            if d < STREAMED:
                mode = "stream"
            else:
                mode = "load" if held[d] is query_grads else "held"
            images, *block = images_of_query(
                where, d, mine, other, held[d], mode, d % 2, 2, earlier
            )
            held[d] = block[0] if block else held[d]
            done.append(images)

        gathered(piece, step)
        return [par_pair(part) for part in done[1::2]]

    def basis_from(pairs):
        images, gram = local_gram(where, pairs)
        gram = gram + tok_swap(gram, 1)
        others = [tok_swap(gram, CORES * d) for d in range(1, chips)]
        return orthonormal(images, [gram] + others)

    def back_piece(basis):
        after, arrived, total = [], [], None
        for d in reversed(range(chips)):
            mine, other = back_of_query(where, d, basis, held[d], after)
            after = [other]
            total = mine + tok_swap(other, 1).astype(F32)
            if d:
                arrived.append(tok_swap(total.astype(BF16), CORES * d))
        for part in arrived:
            total = total + part.astype(F32)
        return total.astype(BF16)

    piece = start_block.T
    basis = None
    for _ in range(ITERS):
        basis = basis_from(images_from(piece))
        piece = back_piece(basis)

    got = flat = basis.reshape(queries * RANK, rows)
    owners = [0]
    for bits in [1 << i for i in reversed(range(chips.bit_length() - 1))]:
        sends = [
            (((p ^ o) * CORES + c) * pars + p, ((p ^ o ^ bits) * CORES + c) * pars + p)
            for p in range(pars)
            for o in owners
            for c in range(CORES)
        ]
        received = lax.ppermute(got, ("tok", "par"), sends)
        got = choose(where, got, received, owners)
        owners = owners + [o ^ bits for o in owners]
    out_proj = project_out(where, got, tok_swap(got, 1), hooked_out)

    parts = []

    def in_proj(d, mine, other):
        earlier = parts[-1] if d > 1 else None
        slot, slots = max(d - 1, 0), chips - 1 if d else 1
        parts.append(project_in(where, mine, other, hooked_in, slot, slots, earlier))

    gathered(piece, in_proj)
    pairs = [par_pair(out_proj), par_pair(parts[0]), par_pair(parts[-1])]
    return token_scores(where, pairs)


def plain(query_grads, start_block, hooked_out, hooked_in):
    queries, rows_tok = query_grads.shape[:2]
    cols_par = hooked_out.shape[1]

    def blocked(x):
        return x.reshape(x.shape[0], queries, RANK)

    subspace = lax.all_gather(start_block, "tok", axis=1, tiled=True)
    basis = None
    for _ in range(ITERS):
        partial = jnp.einsum(
            "qoi,iqr->oqr", query_grads, blocked(subspace), preferred_element_type=F32
        )
        images = lax.psum(partial.reshape(rows_tok, queries * RANK), "par")
        blocks = blocked(images)
        gram = lax.psum(jnp.einsum("oqr,oqs->qrs", blocks, blocks, precision=HIGH), "tok")
        solved = lax.linalg.triangular_solve(
            jnp.linalg.cholesky(gram), jnp.transpose(blocks, (1, 2, 0)), left_side=True, lower=True
        )
        basis = jnp.transpose(solved, (2, 0, 1)).reshape(images.shape).astype(BF16)
        back = jnp.einsum(
            "qoi,oqr->iqr", query_grads, blocked(basis), preferred_element_type=F32
        )
        subspace = lax.psum(back.reshape(back.shape[0], queries * RANK), "tok").astype(BF16)
    gathered = lax.all_gather(basis, "tok", axis=0, tiled=True)
    basis_par = lax.dynamic_slice_in_dim(gathered, lax.axis_index("par") * cols_par, cols_par, 0)
    out_proj = jnp.dot(hooked_out, basis_par, preferred_element_type=F32)
    in_proj = jnp.dot(hooked_in, subspace, preferred_element_type=F32)
    whole_out, whole_in = lax.psum((out_proj, in_proj), "par")
    return (whole_out * whole_in).reshape(whole_out.shape[0], queries, RANK).sum(axis=2).T


def solution(mesh):
    toks, pars = mesh.shape["tok"], mesh.shape["par"]
    placed = (P(None, "tok", "par"), P("par", "tok"), P("tok", "par"), P("tok", "par"))

    def mapped(body):
        return jax.shard_map(
            body, mesh=mesh, in_specs=placed, out_specs=P(None, "tok"), check_vma=False
        )

    def suited(queries):
        return toks == CORES * queries == CORES * pars == 8

    paired = mapped(functools.partial(fast, toks=toks, pars=pars))

    def step(query_grads, *others):
        run = paired if suited(query_grads.shape[0]) else mapped(plain)
        return run(query_grads, *others)

    return step
```

```python
import functools
import jax
import jax.numpy as jnp
from jax import lax
from jax.experimental import pallas as pl
from jax.experimental.pallas import tpu as pltpu
from jax.sharding import PartitionSpec as P

RANK = 32
ITERS = 2
CORES = 2
F32, BF16 = jnp.float32, jnp.bfloat16
HIGH = lax.Precision.HIGHEST
NT = (((1,), (1,)), ((), ()))
ANY = pl.BlockSpec(memory_space=pl.ANY)
VMEM = pl.BlockSpec(memory_space=pltpu.VMEM)
SMEM = pl.BlockSpec(memory_space=pltpu.SMEM)
MIB = 1024 * 1024


def params(mebibytes=1):
    return pltpu.CompilerParams(vmem_limit_bytes=mebibytes * MIB)


def cost(flops, nbytes):
    return pl.CostEstimate(flops=int(flops), bytes_accessed=int(nbytes), transcendentals=0)


def both_cores(core, mine, other, axis):
    return jnp.concatenate(
        [jnp.where(core == 0, mine, other), jnp.where(core == 0, other, mine)], axis=axis
    )


ROW_CHUNKS = 4
COL_CHUNKS = 8
STREAM_BANDS = 2
STREAM_COLS = 4
STREAM_MIB = 9


def images_body(where, mine_ref, other_ref, *refs, carried, mode, offset):
    refs = list(refs)
    carry_ref = refs.pop(0) if carried else None
    source_ref, out_ref = refs.pop(0), refs.pop(0)
    query, core = where[0] ^ offset, where[1]
    rows = out_ref.shape[1] // ROW_CHUNKS
    ahead = STREAM_BANDS if mode == "stream" else ROW_CHUNKS

    def band(i):
        return pl.ds(pl.multiple_of(i * rows, 128), rows)

    def view(i):
        if mode == "stream":
            return refs[0].at[lax.rem(i, STREAM_BANDS)]
        return (source_ref if mode == "held" else refs[0]).at[band(i), :]

    def fetch(i):
        return pltpu.make_async_copy(source_ref.at[query, band(i), :], view(i), refs[1].at[i])

    for i in range(0 if mode == "held" else ahead):
        fetch(i).start()
    if carried:
        out_ref[:carried] = carry_ref[...]
    vectors = both_cores(core, mine_ref[...], other_ref[...], 0)

    def body(i, carry):
        if mode != "held":
            fetch(i).wait()
        out_ref[carried:, band(i)] = lax.dot_general(
            vectors, view(i)[...], NT, preferred_element_type=F32
        )
        if mode == "stream":

            @pl.when(i + ahead < ROW_CHUNKS)
            def _():
                fetch(i + ahead).start()

        return carry

    lax.fori_loop(0, ROW_CHUNKS, body, 0)


def images_of_query(where, offset, mine, other, carry, source, mode):
    rows, cols = source.shape[-2:]
    carried = carry.shape[0] if carry is not None else 0
    load = mode == "load"
    scratch = []
    if mode == "stream":
        scratch.append(pltpu.VMEM((STREAM_BANDS, rows // ROW_CHUNKS, cols), BF16))
    if mode != "held":
        scratch.append(pltpu.SemaphoreType.DMA((ROW_CHUNKS,)))
    return pl.pallas_call(
        functools.partial(images_body, carried=carried, mode=mode, offset=offset),
        in_specs=[SMEM, VMEM, VMEM]
        + [VMEM] * bool(carried)
        + [VMEM if mode == "held" else ANY],
        out_specs=[VMEM] * (1 + load),
        out_shape=[jax.ShapeDtypeStruct((carried + RANK, rows), F32)]
        + [pltpu.VMEM((rows, cols), BF16)] * load,
        scratch_shapes=scratch,
        cost_estimate=cost(2 * RANK * rows * cols * 8, 2 * rows * cols),
        compiler_params=params(STREAM_MIB if mode == "stream" else 1),
    )(where, mine, other, *([carry] if carried else []), source)


def back_body(where, basis_ref, source_ref, *rest, stream, ties, offset):
    mine_ref, other_ref, *rest = rest[ties:]
    query, core = where[0] ^ offset, where[1]
    half = mine_ref.shape[0]
    width = mine_ref.shape[1] // COL_CHUNKS
    vectors = basis_ref[query]

    def band(i):
        return pl.ds(pl.multiple_of(i * width, 128), width)

    def view(i):
        return rest[0].at[lax.rem(i, STREAM_COLS)] if stream else source_ref.at[:, band(i)]

    def fetch(i):
        return pltpu.make_async_copy(source_ref.at[query, :, band(i)], view(i), rest[1].at[i])

    for i in range(STREAM_COLS if stream else 0):
        fetch(i).start()

    def body(i, carry):
        if stream:
            fetch(i).wait()
        product = jnp.dot(vectors, view(i)[...], preferred_element_type=F32)
        low, high = product[:half], product[half:]
        mine_ref[:, band(i)] = jnp.where(core == 0, low, high)
        other_ref[:, band(i)] = jnp.where(core == 0, high, low).astype(BF16)
        if stream:

            @pl.when(i + STREAM_COLS < COL_CHUNKS)
            def _():
                fetch(i + STREAM_COLS).start()

        return carry

    lax.fori_loop(0, COL_CHUNKS, body, 0)


def back_of_query(where, offset, basis, source, after):
    rows, cols = source.shape[-2:]
    stream = source.ndim == 3
    half = RANK // CORES
    scratch = [
        pltpu.VMEM((STREAM_COLS, rows, cols // COL_CHUNKS), BF16),
        pltpu.SemaphoreType.DMA((COL_CHUNKS,)),
    ]
    return pl.pallas_call(
        functools.partial(back_body, stream=stream, ties=len(after), offset=offset),
        in_specs=[SMEM, VMEM, ANY if stream else VMEM] + [ANY] * len(after),
        out_specs=[VMEM, VMEM],
        out_shape=[
            jax.ShapeDtypeStruct((half, cols), F32),
            jax.ShapeDtypeStruct((half, cols), BF16),
        ],
        scratch_shapes=scratch if stream else [],
        cost_estimate=cost(2 * RANK * rows * cols * 8, 2 * rows * cols),
        compiler_params=params(STREAM_MIB if stream else 1),
    )(where, basis, source, *after)


def total_body(*refs):
    value = refs[0][...].astype(F32)
    for ref in refs[1:-1]:
        value = value + ref[...].astype(F32)
    refs[-1][...] = value.astype(refs[-1].dtype)


def total(parts, dtype=F32):
    return pl.pallas_call(
        total_body,
        in_specs=[VMEM] * len(parts),
        out_specs=VMEM,
        out_shape=jax.ShapeDtypeStruct(parts[0].shape, dtype),
        cost_estimate=cost(len(parts) * parts[0].size, 4 * len(parts) * parts[0].size),
        compiler_params=params(),
    )(*parts)


def gram_body(where, *refs):
    pairs, (images_ref, gram_ref) = refs[:-2], refs[-2:]
    queries = images_ref.shape[0]
    d = 0
    for held, received in zip(pairs[0::2], pairs[1::2]):
        for start in range(0, held.shape[0], RANK):
            block = pl.ds(start, RANK)
            images_ref[where[0] ^ d] = held[block, :] + received[block, :]
            d += 1
    for query in range(queries):
        block = images_ref[query]
        gram_ref[:, query * RANK : (query + 1) * RANK] = lax.dot_general(
            block, block, NT, precision=HIGH, preferred_element_type=F32
        )


def local_gram(where, pairs):
    flat = [part for pair in pairs for part in pair]
    rows = flat[0].shape[1]
    queries = sum(held.shape[0] for held, _ in pairs) // RANK
    return pl.pallas_call(
        gram_body,
        in_specs=[SMEM] + [VMEM] * len(flat),
        out_specs=[VMEM, VMEM],
        out_shape=[
            jax.ShapeDtypeStruct((queries, RANK, rows), F32),
            jax.ShapeDtypeStruct((RANK, queries * RANK), F32),
        ],
        cost_estimate=cost(12 * RANK * RANK * queries * rows, 16 * queries * RANK * rows),
        compiler_params=params(),
    )(where, *flat)


def basis_body(images_ref, *refs):
    gram_refs, basis_ref = refs[:-1], refs[-1]
    queries = images_ref.shape[0]
    total = queries * RANK
    gram = gram_refs[0][...]
    for ref in gram_refs[1:]:
        gram = gram + ref[...]
    stacked = jnp.concatenate(
        [gram[:, q * RANK : (q + 1) * RANK] for q in range(queries)], axis=0
    )
    row = lax.broadcasted_iota(jnp.int32, (total, RANK), 0) % RANK
    col = lax.broadcasted_iota(jnp.int32, (total, RANK), 1)
    table = jnp.concatenate([stacked, jnp.where(row == col, 1.0, 0.0).astype(F32)], axis=1)
    row = lax.broadcasted_iota(jnp.int32, (total, 2 * RANK), 0) % RANK
    table = table.reshape(queries, RANK, 2 * RANK)
    row = row.reshape(queries, RANK, 2 * RANK)
    scales = jnp.zeros((queries, RANK, 1), F32)
    for k in range(RANK):
        pivot_row = table[:, k : k + 1, :]
        pivot = pivot_row[:, :, k : k + 1]
        factor = table[:, :, k : k + 1] / pivot
        scales = jnp.where(row[:, :, :1] == k, lax.rsqrt(pivot), scales)
        table = table - jnp.where(row > k, factor * pivot_row, 0.0)
    inverse = table[:, :, RANK:] * scales
    for q in range(queries):
        basis_ref[q] = jnp.dot(
            inverse[q], images_ref[q], precision=HIGH, preferred_element_type=F32
        ).astype(BF16)


def orthonormal(images, grams):
    return pl.pallas_call(
        basis_body,
        in_specs=[VMEM] * (1 + len(grams)),
        out_specs=VMEM,
        out_shape=jax.ShapeDtypeStruct(images.shape, BF16),
        cost_estimate=cost(12 * RANK * images.size + 10**9, 6 * images.size),
        compiler_params=params(),
    )(images, *grams)


def choose_body(where, held_ref, received_ref, out_ref, *, owners):
    wanted = where[2]
    own = functools.reduce(jnp.logical_or, [where[0] == wanted ^ bits for bits in owners])
    out_ref[...] = jnp.where(own, held_ref[...], received_ref[...])


def choose(where, held, received, owners):
    return pl.pallas_call(
        functools.partial(choose_body, owners=owners),
        in_specs=[SMEM, VMEM, VMEM],
        out_specs=VMEM,
        out_shape=jax.ShapeDtypeStruct(held.shape, held.dtype),
        cost_estimate=cost(held.size, 6 * held.size),
        compiler_params=params(),
    )(where, held, received)


def project_out_body(where, mine_ref, other_ref, hooked_ref, out_ref, scratch):
    vectors = both_cores(where[1], mine_ref[...], other_ref[...], 1)
    queries = scratch.shape[0]
    scratch[...] = lax.dot_general(
        vectors, hooked_ref[...], NT, preferred_element_type=F32
    ).reshape(scratch.shape)
    for d in range(queries):
        out_ref[d] = scratch[where[0] ^ d]


def project_out(where, mine, other, hooked):
    shape = (mine.shape[0] // RANK, RANK, hooked.shape[0])
    return pl.pallas_call(
        project_out_body,
        in_specs=[SMEM, VMEM, VMEM, VMEM],
        out_specs=VMEM,
        out_shape=jax.ShapeDtypeStruct(shape, F32),
        scratch_shapes=[pltpu.VMEM(shape, F32)],
        cost_estimate=cost(4 * mine.size * hooked.shape[0], 2 * hooked.size),
        compiler_params=params(4),
    )(where, mine, other, hooked)


def project_in_body(where, mine_ref, other_ref, hooked_ref, *rest):
    vectors = both_cores(where[1], mine_ref[...], other_ref[...], 0)
    rest[-1][0] = lax.dot_general(vectors, hooked_ref[...], NT, preferred_element_type=F32)


def project_in(where, mine, other, hooked, slot, slots, earlier=None):
    tokens = hooked.shape[0]
    aliased = earlier is not None
    return pl.pallas_call(
        project_in_body,
        grid=(1,),
        in_specs=[SMEM, VMEM, VMEM, VMEM] + [ANY] * aliased,
        out_specs=pl.BlockSpec((1, RANK, tokens), lambda i: (slot, 0, 0)),
        out_shape=jax.ShapeDtypeStruct((slots, RANK, tokens), F32),
        input_output_aliases={4: 0} if aliased else {},
        cost_estimate=cost(4 * mine.size * tokens, 2 * hooked.size),
        compiler_params=params(8),
    )(where, mine, other, hooked, *([earlier] if aliased else []))


def scores_body(where, *refs):
    sums, score_ref = [], refs[-1]
    for held_ref, received_ref in zip(refs[:-1:2], refs[1:-1:2]):
        sums += [held_ref[i] + received_ref[i] for i in range(held_ref.shape[0])]
    queries = len(sums) // 2
    for d in range(queries):
        score = (sums[d] * sums[queries + d]).sum(axis=0, keepdims=True)
        score_ref[pl.ds(where[0] ^ d, 1), :] = score


def token_scores(where, pairs):
    flat = [part for pair in pairs for part in pair]
    queries = sum(held.shape[0] for held, _ in pairs) // 2
    return pl.pallas_call(
        scores_body,
        in_specs=[SMEM] + [VMEM] * len(flat),
        out_specs=VMEM,
        out_shape=jax.ShapeDtypeStruct((queries, flat[0].shape[2]), F32),
        compiler_params=params(),
    )(where, *flat)


def xor_permute(x, axis, size, bits):
    return lax.ppermute(x, axis, [(i, i ^ bits) for i in range(size)])


def fast(query_grads, start_block, hooked_out, hooked_in, *, toks, pars):
    queries, rows, _ = query_grads.shape
    chips = toks // CORES
    tok, par = lax.axis_index("tok"), lax.axis_index("par")
    chip, core = tok // CORES, tok % CORES
    where = jnp.stack([chip, core, par]).astype(jnp.int32)
    par_bits = [1 << i for i in range(pars.bit_length() - 1)]
    held = [query_grads] + [None] * (chips - 1)

    def tok_swap(x, bits):
        return xor_permute(x, "tok", toks, bits)

    def par_pair(x):
        for b in par_bits[:-1]:
            received = xor_permute(x, "par", pars, b)
            x = total([x, received])
        return x, xor_permute(x, "par", pars, par_bits[-1])

    def gathered(piece, step):
        pieces = [piece] + [tok_swap(piece, CORES * d) for d in range(1, chips)]
        for d in range(chips):
            other = tok_swap(pieces[d], 1)
            step(d, pieces[d], other)

    def images_from(piece):
        pairs, carry = [], None

        def step(d, mine, other):
            nonlocal carry
            source, mode = held[d], "held" if d else "stream"
            if source is None:
                source, mode = query_grads, "load"
            images, *block = images_of_query(where, d, mine, other, carry, source, mode)
            held[d] = block[0] if block else held[d]
            carry = images if d in JOINED else None
            if carry is None:
                pairs.append(par_pair(images))

        gathered(piece, step)
        return pairs

    def basis_from(pairs):
        images, gram = local_gram(where, pairs)
        gram = total([gram, tok_swap(gram, 1)])
        others = [tok_swap(gram, CORES * d) for d in range(1, chips)]
        return orthonormal(images, [gram] + others)

    def back_piece(basis):
        after, arrived = [], []
        for d in reversed(range(chips)):
            mine, other = back_of_query(where, d, basis, held[d], after)
            after = [other]
            received = tok_swap(other, 1)
            if d:
                arrived.append(tok_swap(total([mine, received], BF16), CORES * d))
        return total([mine, received] + arrived, BF16)

    def spread(basis):
        got = basis.reshape(queries * RANK, rows)
        owners = [0]
        for bits in [1 << i for i in reversed(range(chips.bit_length() - 1))]:
            sends = [
                (((p ^ o) * CORES + c) * pars + p, ((p ^ o ^ bits) * CORES + c) * pars + p)
                for p in range(pars)
                for o in owners
                for c in range(CORES)
            ]
            received = lax.ppermute(got, ("tok", "par"), sends)
            got = choose(where, got, received, owners)
            owners = owners + [o ^ bits for o in owners]
        return got

    piece = start_block.T
    for i in range(ITERS):
        basis = basis_from(images_from(piece))
        if i == ITERS - 1:
            spread_rows = spread(basis)
        piece = back_piece(basis)

    parts = []

    def in_proj(d, mine, other):
        last = d == chips - 1
        earlier = parts[-1] if 0 < d and not last else None
        slot, slots = (0, 1) if last else (d, chips - 1)
        parts.append(project_in(where, mine, other, hooked_in, slot, slots, earlier))

    gathered(piece, in_proj)
    other_rows = tok_swap(spread_rows, 1)
    out_proj = project_out(where, spread_rows, other_rows, hooked_out)
    pairs = [par_pair(out_proj), par_pair(parts[-2]), par_pair(parts[-1])]
    return token_scores(where, pairs)


JOINED = (0,)


def plain(query_grads, start_block, hooked_out, hooked_in):
    queries, rows_tok = query_grads.shape[:2]
    cols_par = hooked_out.shape[1]

    def blocked(x):
        return x.reshape(x.shape[0], queries, RANK)

    subspace = lax.all_gather(start_block, "tok", axis=1, tiled=True)
    basis = None
    for _ in range(ITERS):
        partial = jnp.einsum(
            "qoi,iqr->oqr", query_grads, blocked(subspace), preferred_element_type=F32
        )
        images = lax.psum(partial.reshape(rows_tok, queries * RANK), "par")
        blocks = blocked(images)
        gram = lax.psum(jnp.einsum("oqr,oqs->qrs", blocks, blocks, precision=HIGH), "tok")
        solved = lax.linalg.triangular_solve(
            jnp.linalg.cholesky(gram), jnp.transpose(blocks, (1, 2, 0)), left_side=True, lower=True
        )
        basis = jnp.transpose(solved, (2, 0, 1)).reshape(images.shape).astype(BF16)
        back = jnp.einsum(
            "qoi,oqr->iqr", query_grads, blocked(basis), preferred_element_type=F32
        )
        subspace = lax.psum(back.reshape(back.shape[0], queries * RANK), "tok").astype(BF16)
    gathered = lax.all_gather(basis, "tok", axis=0, tiled=True)
    basis_par = lax.dynamic_slice_in_dim(gathered, lax.axis_index("par") * cols_par, cols_par, 0)
    out_proj = jnp.dot(hooked_out, basis_par, preferred_element_type=F32)
    in_proj = jnp.dot(hooked_in, subspace, preferred_element_type=F32)
    whole_out, whole_in = lax.psum((out_proj, in_proj), "par")
    return (whole_out * whole_in).reshape(whole_out.shape[0], queries, RANK).sum(axis=2).T


def solution(mesh):
    toks, pars = mesh.shape["tok"], mesh.shape["par"]
    placed = (P(None, "tok", "par"), P("par", "tok"), P("tok", "par"), P("tok", "par"))

    def mapped(body):
        return jax.shard_map(
            body, mesh=mesh, in_specs=placed, out_specs=P(None, "tok"), check_vma=False
        )

    def suited(queries):
        return toks == CORES * queries == CORES * pars == 8

    paired = mapped(functools.partial(fast, toks=toks, pars=pars))

    def step(query_grads, *others):
        run = paired if suited(query_grads.shape[0]) else mapped(plain)
        return run(query_grads, *others)

    return step
```

```python
import functools
import jax
import jax.numpy as jnp
from jax import lax
from jax.experimental import pallas as pl
from jax.experimental.pallas import tpu as pltpu
from jax.sharding import PartitionSpec as P

RANK = 32
ITERS = 2
CORES = 2
F32, BF16 = jnp.float32, jnp.bfloat16
HIGH = lax.Precision.HIGHEST
NT = (((1,), (1,)), ((), ()))
ANY = pl.BlockSpec(memory_space=pl.ANY)
VMEM = pl.BlockSpec(memory_space=pltpu.VMEM)
SMEM = pl.BlockSpec(memory_space=pltpu.SMEM)
MIB = 1024 * 1024


def params(mebibytes=1):
    return pltpu.CompilerParams(vmem_limit_bytes=mebibytes * MIB)


def cost(flops, nbytes):
    return pl.CostEstimate(flops=int(flops), bytes_accessed=int(nbytes), transcendentals=0)


def both_cores(core, mine, other, axis):
    return jnp.concatenate(
        [jnp.where(core == 0, mine, other), jnp.where(core == 0, other, mine)], axis=axis
    )


ROW_CHUNKS = 4
COL_CHUNKS = 8
AHEAD = 2
STREAM_COLS = 4
STREAM_MIB = 9


def images_body(where, mine_ref, other_ref, *refs, carried, mode, offset):
    refs = list(refs)
    carry_ref = refs.pop(0) if carried else None
    source_ref, out_ref = refs.pop(0), refs.pop(0)
    query, core = where[0] ^ offset, where[1]
    rows = out_ref.shape[1] // ROW_CHUNKS
    ahead = AHEAD

    def band(i):
        return pl.ds(pl.multiple_of(i * rows, 128), rows)

    def view(i):
        if mode == "stream":
            return refs[0].at[lax.rem(i, ahead)]
        return (source_ref if mode == "held" else refs[0]).at[band(i), :]

    def fetch(i):
        return pltpu.make_async_copy(source_ref.at[query, band(i), :], view(i), refs[1].at[i])

    for i in range(0 if mode == "held" else ahead):
        fetch(i).start()
    if carried:
        out_ref[:carried] = carry_ref[...]
    vectors = both_cores(core, mine_ref[...], other_ref[...], 0)

    def body(i, carry):
        if mode != "held":
            fetch(i).wait()
        if mode == "load":

            @pl.when(i + ahead < ROW_CHUNKS)
            def _():
                fetch(i + ahead).start()

        out_ref[carried:, band(i)] = lax.dot_general(
            vectors, view(i)[...], NT, preferred_element_type=F32
        )
        if mode == "stream":

            @pl.when(i + ahead < ROW_CHUNKS)
            def _():
                fetch(i + ahead).start()

        return carry

    lax.fori_loop(0, ROW_CHUNKS, body, 0)


def images_of_query(where, offset, mine, other, carry, source, mode):
    rows, cols = source.shape[-2:]
    carried = carry.shape[0] if carry is not None else 0
    load = mode == "load"
    scratch = []
    if mode == "stream":
        scratch.append(pltpu.VMEM((AHEAD, rows // ROW_CHUNKS, cols), BF16))
    if mode != "held":
        scratch.append(pltpu.SemaphoreType.DMA((ROW_CHUNKS,)))
    return pl.pallas_call(
        functools.partial(images_body, carried=carried, mode=mode, offset=offset),
        in_specs=[SMEM, VMEM, VMEM]
        + [VMEM] * bool(carried)
        + [VMEM if mode == "held" else ANY],
        out_specs=[VMEM] * (1 + load),
        out_shape=[jax.ShapeDtypeStruct((carried + RANK, rows), F32)]
        + [pltpu.VMEM((rows, cols), BF16)] * load,
        scratch_shapes=scratch,
        cost_estimate=cost(2 * RANK * rows * cols * 8, 2 * rows * cols),
        compiler_params=params(STREAM_MIB if mode == "stream" else 1),
    )(where, mine, other, *([carry] if carried else []), source)


def back_body(where, basis_ref, source_ref, *rest, stream, ties, offset):
    mine_ref, other_ref, *rest = rest[ties:]
    query, core = where[0] ^ offset, where[1]
    half = mine_ref.shape[0]
    width = mine_ref.shape[1] // COL_CHUNKS
    vectors = basis_ref[query]

    def band(i):
        return pl.ds(pl.multiple_of(i * width, 128), width)

    def view(i):
        return rest[0].at[lax.rem(i, STREAM_COLS)] if stream else source_ref.at[:, band(i)]

    def fetch(i):
        return pltpu.make_async_copy(source_ref.at[query, :, band(i)], view(i), rest[1].at[i])

    for i in range(STREAM_COLS if stream else 0):
        fetch(i).start()

    def body(i, carry):
        if stream:
            fetch(i).wait()
        product = jnp.dot(vectors, view(i)[...], preferred_element_type=F32)
        low, high = product[:half], product[half:]
        mine_ref[:, band(i)] = jnp.where(core == 0, low, high)
        other_ref[:, band(i)] = jnp.where(core == 0, high, low).astype(BF16)
        if stream:

            @pl.when(i + STREAM_COLS < COL_CHUNKS)
            def _():
                fetch(i + STREAM_COLS).start()

        return carry

    lax.fori_loop(0, COL_CHUNKS, body, 0)


def back_of_query(where, offset, basis, source, after):
    rows, cols = source.shape[-2:]
    stream = source.ndim == 3
    half = RANK // CORES
    scratch = [
        pltpu.VMEM((STREAM_COLS, rows, cols // COL_CHUNKS), BF16),
        pltpu.SemaphoreType.DMA((COL_CHUNKS,)),
    ]
    return pl.pallas_call(
        functools.partial(back_body, stream=stream, ties=len(after), offset=offset),
        in_specs=[SMEM, VMEM, ANY if stream else VMEM] + [ANY] * len(after),
        out_specs=[VMEM, VMEM],
        out_shape=[
            jax.ShapeDtypeStruct((half, cols), F32),
            jax.ShapeDtypeStruct((half, cols), BF16),
        ],
        scratch_shapes=scratch if stream else [],
        cost_estimate=cost(2 * RANK * rows * cols * 8, 2 * rows * cols),
        compiler_params=params(STREAM_MIB if stream else 1),
    )(where, basis, source, *after)


def total_body(*refs):
    value = refs[0][...].astype(F32)
    for ref in refs[1:-1]:
        value = value + ref[...].astype(F32)
    refs[-1][...] = value.astype(refs[-1].dtype)


def total(parts, dtype=F32):
    return pl.pallas_call(
        total_body,
        in_specs=[VMEM] * len(parts),
        out_specs=VMEM,
        out_shape=jax.ShapeDtypeStruct(parts[0].shape, dtype),
        cost_estimate=cost(len(parts) * parts[0].size, 4 * len(parts) * parts[0].size),
        compiler_params=params(),
    )(*parts)


def gram_body(where, *refs):
    pairs, (images_ref, gram_ref) = refs[:-2], refs[-2:]
    queries = images_ref.shape[0]
    d = 0
    for held, received in zip(pairs[0::2], pairs[1::2]):
        for start in range(0, held.shape[0], RANK):
            block = pl.ds(start, RANK)
            images_ref[where[0] ^ d] = held[block, :] + received[block, :]
            d += 1
    for query in range(queries):
        block = images_ref[query]
        gram_ref[:, query * RANK : (query + 1) * RANK] = lax.dot_general(
            block, block, NT, precision=HIGH, preferred_element_type=F32
        )


def local_gram(where, pairs):
    flat = [part for pair in pairs for part in pair]
    rows = flat[0].shape[1]
    queries = sum(held.shape[0] for held, _ in pairs) // RANK
    return pl.pallas_call(
        gram_body,
        in_specs=[SMEM] + [VMEM] * len(flat),
        out_specs=[VMEM, VMEM],
        out_shape=[
            jax.ShapeDtypeStruct((queries, RANK, rows), F32),
            jax.ShapeDtypeStruct((RANK, queries * RANK), F32),
        ],
        cost_estimate=cost(12 * RANK * RANK * queries * rows, 16 * queries * RANK * rows),
        compiler_params=params(),
    )(where, *flat)


def basis_body(images_ref, *refs):
    gram_refs, basis_ref = refs[:-1], refs[-1]
    queries = images_ref.shape[0]
    total = queries * RANK
    gram = gram_refs[0][...]
    for ref in gram_refs[1:]:
        gram = gram + ref[...]
    stacked = jnp.concatenate(
        [gram[:, q * RANK : (q + 1) * RANK] for q in range(queries)], axis=0
    )
    row = lax.broadcasted_iota(jnp.int32, (total, RANK), 0) % RANK
    col = lax.broadcasted_iota(jnp.int32, (total, RANK), 1)
    table = jnp.concatenate([stacked, jnp.where(row == col, 1.0, 0.0).astype(F32)], axis=1)
    row = lax.broadcasted_iota(jnp.int32, (total, 2 * RANK), 0) % RANK
    table = table.reshape(queries, RANK, 2 * RANK)
    row = row.reshape(queries, RANK, 2 * RANK)
    scales = jnp.zeros((queries, RANK, 1), F32)
    for k in range(RANK):
        pivot_row = table[:, k : k + 1, :]
        pivot = pivot_row[:, :, k : k + 1]
        factor = table[:, :, k : k + 1] / pivot
        scales = jnp.where(row[:, :, :1] == k, lax.rsqrt(pivot), scales)
        table = table - jnp.where(row > k, factor * pivot_row, 0.0)
    inverse = table[:, :, RANK:] * scales
    for q in range(queries):
        basis_ref[q] = jnp.dot(
            inverse[q], images_ref[q], precision=HIGH, preferred_element_type=F32
        ).astype(BF16)


def orthonormal(images, grams):
    return pl.pallas_call(
        basis_body,
        in_specs=[VMEM] * (1 + len(grams)),
        out_specs=VMEM,
        out_shape=jax.ShapeDtypeStruct(images.shape, BF16),
        cost_estimate=cost(12 * RANK * images.size + 10**9, 6 * images.size),
        compiler_params=params(),
    )(images, *grams)


def choose_body(where, held_ref, received_ref, out_ref, *, owners):
    wanted = where[2]
    own = functools.reduce(jnp.logical_or, [where[0] == wanted ^ bits for bits in owners])
    out_ref[...] = jnp.where(own, held_ref[...], received_ref[...])


def choose(where, held, received, owners):
    return pl.pallas_call(
        functools.partial(choose_body, owners=owners),
        in_specs=[SMEM, VMEM, VMEM],
        out_specs=VMEM,
        out_shape=jax.ShapeDtypeStruct(held.shape, held.dtype),
        cost_estimate=cost(held.size, 6 * held.size),
        compiler_params=params(),
    )(where, held, received)


def project_out_body(where, mine_ref, other_ref, hooked_ref, out_ref, scratch):
    vectors = both_cores(where[1], mine_ref[...], other_ref[...], 1)
    queries = scratch.shape[0]
    scratch[...] = lax.dot_general(
        vectors, hooked_ref[...], NT, preferred_element_type=F32
    ).reshape(scratch.shape)
    for d in range(queries):
        out_ref[d] = scratch[where[0] ^ d]


def project_out(where, mine, other, hooked):
    shape = (mine.shape[0] // RANK, RANK, hooked.shape[0])
    return pl.pallas_call(
        project_out_body,
        in_specs=[SMEM, VMEM, VMEM, VMEM],
        out_specs=VMEM,
        out_shape=jax.ShapeDtypeStruct(shape, F32),
        scratch_shapes=[pltpu.VMEM(shape, F32)],
        cost_estimate=cost(4 * mine.size * hooked.shape[0], 2 * hooked.size),
        compiler_params=params(4),
    )(where, mine, other, hooked)


def project_in_body(where, mine_ref, other_ref, hooked_ref, *rest):
    vectors = both_cores(where[1], mine_ref[...], other_ref[...], 0)
    rest[-1][0] = lax.dot_general(vectors, hooked_ref[...], NT, preferred_element_type=F32)


def project_in(where, mine, other, hooked, slot, slots, earlier=None):
    tokens = hooked.shape[0]
    aliased = earlier is not None
    return pl.pallas_call(
        project_in_body,
        grid=(1,),
        in_specs=[SMEM, VMEM, VMEM, VMEM] + [ANY] * aliased,
        out_specs=pl.BlockSpec((1, RANK, tokens), lambda i: (slot, 0, 0)),
        out_shape=jax.ShapeDtypeStruct((slots, RANK, tokens), F32),
        input_output_aliases={4: 0} if aliased else {},
        cost_estimate=cost(4 * mine.size * tokens, 2 * hooked.size),
        compiler_params=params(8),
    )(where, mine, other, hooked, *([earlier] if aliased else []))


def scores_body(where, *refs):
    sums, score_ref = [], refs[-1]
    for held_ref, received_ref in zip(refs[:-1:2], refs[1:-1:2]):
        sums += [held_ref[i] + received_ref[i] for i in range(held_ref.shape[0])]
    queries = len(sums) // 2
    for d in range(queries):
        score = (sums[d] * sums[queries + d]).sum(axis=0, keepdims=True)
        score_ref[pl.ds(where[0] ^ d, 1), :] = score


def token_scores(where, pairs):
    flat = [part for pair in pairs for part in pair]
    queries = sum(held.shape[0] for held, _ in pairs) // 2
    return pl.pallas_call(
        scores_body,
        in_specs=[SMEM] + [VMEM] * len(flat),
        out_specs=VMEM,
        out_shape=jax.ShapeDtypeStruct((queries, flat[0].shape[2]), F32),
        compiler_params=params(),
    )(where, *flat)


def xor_permute(x, axis, size, bits):
    return lax.ppermute(x, axis, [(i, i ^ bits) for i in range(size)])


def fast(query_grads, start_block, hooked_out, hooked_in, *, toks, pars):
    queries, rows, _ = query_grads.shape
    chips = toks // CORES
    tok, par = lax.axis_index("tok"), lax.axis_index("par")
    chip, core = tok // CORES, tok % CORES
    where = jnp.stack([chip, core, par]).astype(jnp.int32)
    par_bits = [1 << i for i in range(pars.bit_length() - 1)]
    held = [query_grads] + [None] * (chips - 1)

    def tok_swap(x, bits):
        return xor_permute(x, "tok", toks, bits)

    def par_pair(x):
        for b in par_bits[:-1]:
            received = xor_permute(x, "par", pars, b)
            x = total([x, received])
        return x, xor_permute(x, "par", pars, par_bits[-1])

    def gathered(piece, step):
        pieces = [piece] + [tok_swap(piece, CORES * d) for d in range(1, chips)]
        for d in range(chips):
            other = tok_swap(pieces[d], 1)
            step(d, pieces[d], other)

    def images_from(piece):
        pairs, carry = [], None

        def step(d, mine, other):
            nonlocal carry
            source, mode = held[d], "held" if d else "stream"
            if source is None:
                source, mode = query_grads, "load"
            images, *block = images_of_query(where, d, mine, other, carry, source, mode)
            held[d] = block[0] if block else held[d]
            carry = images if d in JOINED else None
            if carry is None:
                pairs.append(par_pair(images))

        gathered(piece, step)
        return pairs

    def basis_from(pairs):
        images, gram = local_gram(where, pairs)
        gram = total([gram, tok_swap(gram, 1)])
        others = [tok_swap(gram, CORES * d) for d in range(1, chips)]
        return orthonormal(images, [gram] + others)

    def back_piece(basis):
        after, arrived = [], []
        for d in reversed(range(chips)):
            mine, other = back_of_query(where, d, basis, held[d], after)
            after = [other]
            received = tok_swap(other, 1)
            if d:
                arrived.append(tok_swap(total([mine, received], BF16), CORES * d))
        return total([mine, received] + arrived, BF16)

    def spread(basis):
        got = basis.reshape(queries * RANK, rows)
        owners = [0]
        for bits in [1 << i for i in reversed(range(chips.bit_length() - 1))]:
            sends = [
                (((p ^ o) * CORES + c) * pars + p, ((p ^ o ^ bits) * CORES + c) * pars + p)
                for p in range(pars)
                for o in owners
                for c in range(CORES)
            ]
            received = lax.ppermute(got, ("tok", "par"), sends)
            if bits > 1:
                got = chosen(got, received, owners)
                owners = owners + [o ^ bits for o in owners]
        return got, received, owners

    def chosen(got, received, owners):
        return choose(where, got, received, owners)

    piece = start_block.T
    for i in range(ITERS):
        basis = basis_from(images_from(piece))
        if i == ITERS - 1:
            spread_parts = spread(basis)
        piece = back_piece(basis)

    parts = []

    def in_proj(d, mine, other):
        group = chips // 2
        earlier = parts[-1] if d % group else None
        slot, slots = d % group, group
        parts.append(project_in(where, mine, other, hooked_in, slot, slots, earlier))

    gathered(piece, in_proj)
    spread_rows = chosen(*spread_parts)
    other_rows = tok_swap(spread_rows, 1)
    out_proj = project_out(where, spread_rows, other_rows, hooked_out)
    early, late = parts[chips // 2 - 1], parts[-1]
    pairs = [par_pair(out_proj), par_pair(early), par_pair(late)]
    return token_scores(where, pairs)


JOINED = (0,)


def plain(query_grads, start_block, hooked_out, hooked_in):
    queries, rows_tok = query_grads.shape[:2]
    cols_par = hooked_out.shape[1]

    def blocked(x):
        return x.reshape(x.shape[0], queries, RANK)

    subspace = lax.all_gather(start_block, "tok", axis=1, tiled=True)
    basis = None
    for _ in range(ITERS):
        partial = jnp.einsum(
            "qoi,iqr->oqr", query_grads, blocked(subspace), preferred_element_type=F32
        )
        images = lax.psum(partial.reshape(rows_tok, queries * RANK), "par")
        blocks = blocked(images)
        gram = lax.psum(jnp.einsum("oqr,oqs->qrs", blocks, blocks, precision=HIGH), "tok")
        solved = lax.linalg.triangular_solve(
            jnp.linalg.cholesky(gram), jnp.transpose(blocks, (1, 2, 0)), left_side=True, lower=True
        )
        basis = jnp.transpose(solved, (2, 0, 1)).reshape(images.shape).astype(BF16)
        back = jnp.einsum(
            "qoi,oqr->iqr", query_grads, blocked(basis), preferred_element_type=F32
        )
        subspace = lax.psum(back.reshape(back.shape[0], queries * RANK), "tok").astype(BF16)
    gathered = lax.all_gather(basis, "tok", axis=0, tiled=True)
    basis_par = lax.dynamic_slice_in_dim(gathered, lax.axis_index("par") * cols_par, cols_par, 0)
    out_proj = jnp.dot(hooked_out, basis_par, preferred_element_type=F32)
    in_proj = jnp.dot(hooked_in, subspace, preferred_element_type=F32)
    whole_out, whole_in = lax.psum((out_proj, in_proj), "par")
    return (whole_out * whole_in).reshape(whole_out.shape[0], queries, RANK).sum(axis=2).T


def solution(mesh):
    toks, pars = mesh.shape["tok"], mesh.shape["par"]
    placed = (P(None, "tok", "par"), P("par", "tok"), P("tok", "par"), P("tok", "par"))

    def mapped(body):
        return jax.shard_map(
            body, mesh=mesh, in_specs=placed, out_specs=P(None, "tok"), check_vma=False
        )

    def suited(queries):
        return toks == CORES * queries == CORES * pars == 8

    paired = mapped(functools.partial(fast, toks=toks, pars=pars))

    def step(query_grads, *others):
        run = paired if suited(query_grads.shape[0]) else mapped(plain)
        return run(query_grads, *others)

    return step
```

```python
import functools
import jax
import jax.numpy as jnp
from jax import lax
from jax.experimental import pallas as pl
from jax.experimental.pallas import tpu as pltpu
from jax.sharding import PartitionSpec as P

RANK = 32
ITERS = 2
CORES = 2
F32, BF16 = jnp.float32, jnp.bfloat16
HIGH = lax.Precision.HIGHEST
NT = (((1,), (1,)), ((), ()))
ANY = pl.BlockSpec(memory_space=pl.ANY)
VMEM = pl.BlockSpec(memory_space=pltpu.VMEM)
SMEM = pl.BlockSpec(memory_space=pltpu.SMEM)
MIB = 1024 * 1024


def params(mebibytes=1):
    return pltpu.CompilerParams(vmem_limit_bytes=mebibytes * MIB)


def cost(flops, nbytes):
    return pl.CostEstimate(flops=int(flops), bytes_accessed=int(nbytes), transcendentals=0)


def both_cores(core, mine, other, axis):
    return jnp.concatenate(
        [jnp.where(core == 0, mine, other), jnp.where(core == 0, other, mine)], axis=axis
    )


ROW_CHUNKS = 4
COL_CHUNKS = 8
AHEAD = 3
STREAM_COLS = 6
STREAM_MIB = 12


def images_body(where, mine_ref, other_ref, *refs, carried, mode, offset):
    refs = list(refs)
    carry_ref = refs.pop(0) if carried else None
    source_ref, out_ref = refs.pop(0), refs.pop(0)
    query, core = where[0] ^ offset, where[1]
    rows = out_ref.shape[1] // ROW_CHUNKS
    ahead = AHEAD

    def band(i):
        return pl.ds(pl.multiple_of(i * rows, 128), rows)

    def view(i):
        if mode == "stream":
            return refs[0].at[lax.rem(i, ahead)]
        return (source_ref if mode == "held" else refs[0]).at[band(i), :]

    def fetch(i):
        return pltpu.make_async_copy(source_ref.at[query, band(i), :], view(i), refs[1].at[i])

    for i in range(0 if mode == "held" else ahead):
        fetch(i).start()
    if carried:
        out_ref[:carried] = carry_ref[...]
    vectors = both_cores(core, mine_ref[...], other_ref[...], 0)

    def body(i, carry):
        if mode != "held":
            fetch(i).wait()
        if mode == "load":

            @pl.when(i + ahead < ROW_CHUNKS)
            def _():
                fetch(i + ahead).start()

        out_ref[carried:, band(i)] = lax.dot_general(
            vectors, view(i)[...], NT, preferred_element_type=F32
        )
        if mode == "stream":

            @pl.when(i + ahead < ROW_CHUNKS)
            def _():
                fetch(i + ahead).start()

        return carry

    lax.fori_loop(0, ROW_CHUNKS, body, 0)


def images_of_query(where, offset, mine, other, carry, source, mode):
    rows, cols = source.shape[-2:]
    carried = carry.shape[0] if carry is not None else 0
    load = mode == "load"
    scratch = []
    if mode == "stream":
        scratch.append(pltpu.VMEM((AHEAD, rows // ROW_CHUNKS, cols), BF16))
    if mode != "held":
        scratch.append(pltpu.SemaphoreType.DMA((ROW_CHUNKS,)))
    return pl.pallas_call(
        functools.partial(images_body, carried=carried, mode=mode, offset=offset),
        in_specs=[SMEM, VMEM, VMEM]
        + [VMEM] * bool(carried)
        + [VMEM if mode == "held" else ANY],
        out_specs=[VMEM] * (1 + load),
        out_shape=[jax.ShapeDtypeStruct((carried + RANK, rows), F32)]
        + [pltpu.VMEM((rows, cols), BF16)] * load,
        scratch_shapes=scratch,
        cost_estimate=cost(2 * RANK * rows * cols * 8, 2 * rows * cols),
        compiler_params=params(STREAM_MIB if mode == "stream" else 1),
    )(where, mine, other, *([carry] if carried else []), source)


def back_body(where, basis_ref, source_ref, *rest, stream, ties, offset):
    mine_ref, other_ref, *rest = rest[ties:]
    query, core = where[0] ^ offset, where[1]
    half = mine_ref.shape[0]
    width = mine_ref.shape[1] // COL_CHUNKS
    vectors = basis_ref[query]

    def band(i):
        return pl.ds(pl.multiple_of(i * width, 128), width)

    def view(i):
        return rest[0].at[lax.rem(i, STREAM_COLS)] if stream else source_ref.at[:, band(i)]

    def fetch(i):
        return pltpu.make_async_copy(source_ref.at[query, :, band(i)], view(i), rest[1].at[i])

    for i in range(STREAM_COLS if stream else 0):
        fetch(i).start()

    def body(i, carry):
        if stream:
            fetch(i).wait()
        product = jnp.dot(vectors, view(i)[...], preferred_element_type=F32)
        low, high = product[:half], product[half:]
        mine_ref[:, band(i)] = jnp.where(core == 0, low, high)
        other_ref[:, band(i)] = jnp.where(core == 0, high, low).astype(BF16)
        if stream:

            @pl.when(i + STREAM_COLS < COL_CHUNKS)
            def _():
                fetch(i + STREAM_COLS).start()

        return carry

    lax.fori_loop(0, COL_CHUNKS, body, 0)


def back_of_query(where, offset, basis, source, after):
    rows, cols = source.shape[-2:]
    stream = source.ndim == 3
    half = RANK // CORES
    scratch = [
        pltpu.VMEM((STREAM_COLS, rows, cols // COL_CHUNKS), BF16),
        pltpu.SemaphoreType.DMA((COL_CHUNKS,)),
    ]
    return pl.pallas_call(
        functools.partial(back_body, stream=stream, ties=len(after), offset=offset),
        in_specs=[SMEM, VMEM, ANY if stream else VMEM] + [ANY] * len(after),
        out_specs=[VMEM, VMEM],
        out_shape=[
            jax.ShapeDtypeStruct((half, cols), F32),
            jax.ShapeDtypeStruct((half, cols), BF16),
        ],
        scratch_shapes=scratch if stream else [],
        cost_estimate=cost(2 * RANK * rows * cols * 8, 2 * rows * cols),
        compiler_params=params(STREAM_MIB if stream else 1),
    )(where, basis, source, *after)


def total_body(*refs):
    value = refs[0][...].astype(F32)
    for ref in refs[1:-1]:
        value = value + ref[...].astype(F32)
    refs[-1][...] = value.astype(refs[-1].dtype)


def total(parts, dtype=F32):
    return pl.pallas_call(
        total_body,
        in_specs=[VMEM] * len(parts),
        out_specs=VMEM,
        out_shape=jax.ShapeDtypeStruct(parts[0].shape, dtype),
        cost_estimate=cost(len(parts) * parts[0].size, 4 * len(parts) * parts[0].size),
        compiler_params=params(),
    )(*parts)


def gram_body(where, *refs):
    pairs, (images_ref, gram_ref) = refs[:-2], refs[-2:]
    queries = images_ref.shape[0]
    d = 0
    for held, received in zip(pairs[0::2], pairs[1::2]):
        for start in range(0, held.shape[0], RANK):
            block = pl.ds(start, RANK)
            images_ref[where[0] ^ d] = held[block, :] + received[block, :]
            d += 1
    for query in range(queries):
        block = images_ref[query]
        gram_ref[:, query * RANK : (query + 1) * RANK] = lax.dot_general(
            block, block, NT, precision=HIGH, preferred_element_type=F32
        )


def local_gram(where, pairs):
    flat = [part for pair in pairs for part in pair]
    rows = flat[0].shape[1]
    queries = sum(held.shape[0] for held, _ in pairs) // RANK
    return pl.pallas_call(
        gram_body,
        in_specs=[SMEM] + [VMEM] * len(flat),
        out_specs=[VMEM, VMEM],
        out_shape=[
            jax.ShapeDtypeStruct((queries, RANK, rows), F32),
            jax.ShapeDtypeStruct((RANK, queries * RANK), F32),
        ],
        cost_estimate=cost(12 * RANK * RANK * queries * rows, 16 * queries * RANK * rows),
        compiler_params=params(),
    )(where, *flat)


def basis_body(images_ref, *refs):
    gram_refs, basis_ref = refs[:-1], refs[-1]
    queries = images_ref.shape[0]
    total = queries * RANK
    gram = gram_refs[0][...]
    for ref in gram_refs[1:]:
        gram = gram + ref[...]
    stacked = jnp.concatenate(
        [gram[:, q * RANK : (q + 1) * RANK] for q in range(queries)], axis=0
    )
    row = lax.broadcasted_iota(jnp.int32, (total, RANK), 0) % RANK
    col = lax.broadcasted_iota(jnp.int32, (total, RANK), 1)
    table = jnp.concatenate([stacked, jnp.where(row == col, 1.0, 0.0).astype(F32)], axis=1)
    row = lax.broadcasted_iota(jnp.int32, (total, 2 * RANK), 0) % RANK
    table = table.reshape(queries, RANK, 2 * RANK)
    row = row.reshape(queries, RANK, 2 * RANK)
    scales = jnp.zeros((queries, RANK, 1), F32)
    for k in range(RANK):
        pivot_row = table[:, k : k + 1, :]
        pivot = pivot_row[:, :, k : k + 1]
        factor = table[:, :, k : k + 1] / pivot
        scales = jnp.where(row[:, :, :1] == k, lax.rsqrt(pivot), scales)
        table = table - jnp.where(row > k, factor * pivot_row, 0.0)
    inverse = table[:, :, RANK:] * scales
    for q in range(queries):
        basis_ref[q] = jnp.dot(
            inverse[q], images_ref[q], precision=HIGH, preferred_element_type=F32
        ).astype(BF16)


def orthonormal(images, grams):
    return pl.pallas_call(
        basis_body,
        in_specs=[VMEM] * (1 + len(grams)),
        out_specs=VMEM,
        out_shape=jax.ShapeDtypeStruct(images.shape, BF16),
        cost_estimate=cost(12 * RANK * images.size + 10**9, 6 * images.size),
        compiler_params=params(),
    )(images, *grams)


def choose_body(where, held_ref, received_ref, out_ref, *, owners):
    wanted = where[2]
    own = functools.reduce(jnp.logical_or, [where[0] == wanted ^ bits for bits in owners])
    out_ref[...] = jnp.where(own, held_ref[...], received_ref[...])


def choose(where, held, received, owners):
    return pl.pallas_call(
        functools.partial(choose_body, owners=owners),
        in_specs=[SMEM, VMEM, VMEM],
        out_specs=VMEM,
        out_shape=jax.ShapeDtypeStruct(held.shape, held.dtype),
        cost_estimate=cost(held.size, 6 * held.size),
        compiler_params=params(),
    )(where, held, received)


def project_out_body(where, mine_ref, other_ref, hooked_ref, out_ref, scratch):
    vectors = both_cores(where[1], mine_ref[...], other_ref[...], 1)
    queries = scratch.shape[0]
    scratch[...] = lax.dot_general(
        vectors, hooked_ref[...], NT, preferred_element_type=F32
    ).reshape(scratch.shape)
    for d in range(queries):
        out_ref[d] = scratch[where[0] ^ d]


def project_out(where, mine, other, hooked):
    shape = (mine.shape[0] // RANK, RANK, hooked.shape[0])
    return pl.pallas_call(
        project_out_body,
        in_specs=[SMEM, VMEM, VMEM, VMEM],
        out_specs=VMEM,
        out_shape=jax.ShapeDtypeStruct(shape, F32),
        scratch_shapes=[pltpu.VMEM(shape, F32)],
        cost_estimate=cost(4 * mine.size * hooked.shape[0], 2 * hooked.size),
        compiler_params=params(4),
    )(where, mine, other, hooked)


def project_in_body(where, mine_ref, other_ref, hooked_ref, *rest):
    vectors = both_cores(where[1], mine_ref[...], other_ref[...], 0)
    rest[-1][0] = lax.dot_general(vectors, hooked_ref[...], NT, preferred_element_type=F32)


def project_in(where, mine, other, hooked, slot, slots, earlier=None):
    tokens = hooked.shape[0]
    aliased = earlier is not None
    return pl.pallas_call(
        project_in_body,
        grid=(1,),
        in_specs=[SMEM, VMEM, VMEM, VMEM] + [ANY] * aliased,
        out_specs=pl.BlockSpec((1, RANK, tokens), lambda i: (slot, 0, 0)),
        out_shape=jax.ShapeDtypeStruct((slots, RANK, tokens), F32),
        input_output_aliases={4: 0} if aliased else {},
        cost_estimate=cost(4 * mine.size * tokens, 2 * hooked.size),
        compiler_params=params(8),
    )(where, mine, other, hooked, *([earlier] if aliased else []))


def scores_body(where, *refs):
    sums, score_ref = [], refs[-1]
    for held_ref, received_ref in zip(refs[:-1:2], refs[1:-1:2]):
        sums += [held_ref[i] + received_ref[i] for i in range(held_ref.shape[0])]
    queries = len(sums) // 2
    for d in range(queries):
        score = (sums[d] * sums[queries + d]).sum(axis=0, keepdims=True)
        score_ref[pl.ds(where[0] ^ d, 1), :] = score


def token_scores(where, pairs):
    flat = [part for pair in pairs for part in pair]
    queries = sum(held.shape[0] for held, _ in pairs) // 2
    return pl.pallas_call(
        scores_body,
        in_specs=[SMEM] + [VMEM] * len(flat),
        out_specs=VMEM,
        out_shape=jax.ShapeDtypeStruct((queries, flat[0].shape[2]), F32),
        compiler_params=params(),
    )(where, *flat)


def xor_permute(x, axis, size, bits):
    return lax.ppermute(x, axis, [(i, i ^ bits) for i in range(size)])


def fast(query_grads, start_block, hooked_out, hooked_in, *, toks, pars):
    queries, rows, _ = query_grads.shape
    chips = toks // CORES
    tok, par = lax.axis_index("tok"), lax.axis_index("par")
    chip, core = tok // CORES, tok % CORES
    where = jnp.stack([chip, core, par]).astype(jnp.int32)
    par_bits = [1 << i for i in range(pars.bit_length() - 1)]
    held = [query_grads] + [None] * (chips - 1)

    def tok_swap(x, bits):
        return xor_permute(x, "tok", toks, bits)

    def par_pair(x):
        for b in par_bits[:-1]:
            received = xor_permute(x, "par", pars, b)
            x = total([x, received])
        return x, xor_permute(x, "par", pars, par_bits[-1])

    def gathered(piece, step):
        pieces = [piece] + [tok_swap(piece, CORES * d) for d in range(1, chips)]
        for d in range(chips):
            other = tok_swap(pieces[d], 1)
            step(d, pieces[d], other)

    def images_from(piece):
        pairs, carry = [], None

        def step(d, mine, other):
            nonlocal carry
            source, mode = held[d], "held" if d else "stream"
            if source is None:
                source, mode = query_grads, "load"
            images, *block = images_of_query(where, d, mine, other, carry, source, mode)
            held[d] = block[0] if block else held[d]
            carry = images if d in JOINED else None
            if carry is None:
                pairs.append(par_pair(images))

        gathered(piece, step)
        return pairs

    def basis_from(pairs):
        images, gram = local_gram(where, pairs)
        gram = total([gram, tok_swap(gram, 1)])
        others = [tok_swap(gram, CORES * d) for d in range(1, chips)]
        return orthonormal(images, [gram] + others)

    def back_piece(basis):
        after, arrived = [], []
        for d in reversed(range(chips)):
            mine, other = back_of_query(where, d, basis, held[d], after)
            after = [other]
            received = tok_swap(other, 1)
            if d:
                arrived.append(tok_swap(total([mine, received], BF16), CORES * d))
        return total([mine, received] + arrived, BF16)

    def spread(basis):
        got = basis.reshape(queries * RANK, rows)
        owners = [0]
        for bits in [1 << i for i in reversed(range(chips.bit_length() - 1))]:
            sends = [
                (((p ^ o) * CORES + c) * pars + p, ((p ^ o ^ bits) * CORES + c) * pars + p)
                for p in range(pars)
                for o in owners
                for c in range(CORES)
            ]
            received = lax.ppermute(got, ("tok", "par"), sends)
            if bits > 1:
                got = chosen(got, received, owners)
                owners = owners + [o ^ bits for o in owners]
        return got, received, owners

    def chosen(got, received, owners):
        return choose(where, got, received, owners)

    piece = start_block.T
    for i in range(ITERS):
        basis = basis_from(images_from(piece))
        if i == ITERS - 1:
            spread_parts = spread(basis)
        piece = back_piece(basis)

    parts = []

    def in_proj(d, mine, other):
        group = chips // 2
        earlier = parts[-1] if d % group else None
        slot, slots = d % group, group
        parts.append(project_in(where, mine, other, hooked_in, slot, slots, earlier))

    gathered(piece, in_proj)
    spread_rows = chosen(*spread_parts)
    other_rows = tok_swap(spread_rows, 1)
    out_proj = project_out(where, spread_rows, other_rows, hooked_out)
    early, late = parts[chips // 2 - 1], parts[-1]
    pairs = [par_pair(out_proj), par_pair(early), par_pair(late)]
    return token_scores(where, pairs)


JOINED = (0,)


def plain(query_grads, start_block, hooked_out, hooked_in):
    queries, rows_tok = query_grads.shape[:2]
    cols_par = hooked_out.shape[1]

    def blocked(x):
        return x.reshape(x.shape[0], queries, RANK)

    subspace = lax.all_gather(start_block, "tok", axis=1, tiled=True)
    basis = None
    for _ in range(ITERS):
        partial = jnp.einsum(
            "qoi,iqr->oqr", query_grads, blocked(subspace), preferred_element_type=F32
        )
        images = lax.psum(partial.reshape(rows_tok, queries * RANK), "par")
        blocks = blocked(images)
        gram = lax.psum(jnp.einsum("oqr,oqs->qrs", blocks, blocks, precision=HIGH), "tok")
        solved = lax.linalg.triangular_solve(
            jnp.linalg.cholesky(gram), jnp.transpose(blocks, (1, 2, 0)), left_side=True, lower=True
        )
        basis = jnp.transpose(solved, (2, 0, 1)).reshape(images.shape).astype(BF16)
        back = jnp.einsum(
            "qoi,oqr->iqr", query_grads, blocked(basis), preferred_element_type=F32
        )
        subspace = lax.psum(back.reshape(back.shape[0], queries * RANK), "tok").astype(BF16)
    gathered = lax.all_gather(basis, "tok", axis=0, tiled=True)
    basis_par = lax.dynamic_slice_in_dim(gathered, lax.axis_index("par") * cols_par, cols_par, 0)
    out_proj = jnp.dot(hooked_out, basis_par, preferred_element_type=F32)
    in_proj = jnp.dot(hooked_in, subspace, preferred_element_type=F32)
    whole_out, whole_in = lax.psum((out_proj, in_proj), "par")
    return (whole_out * whole_in).reshape(whole_out.shape[0], queries, RANK).sum(axis=2).T


def solution(mesh):
    toks, pars = mesh.shape["tok"], mesh.shape["par"]
    placed = (P(None, "tok", "par"), P("par", "tok"), P("tok", "par"), P("tok", "par"))

    def mapped(body):
        return jax.shard_map(
            body, mesh=mesh, in_specs=placed, out_specs=P(None, "tok"), check_vma=False
        )

    def suited(queries):
        return toks == CORES * queries == CORES * pars == 8

    paired = mapped(functools.partial(fast, toks=toks, pars=pars))

    def step(query_grads, *others):
        run = paired if suited(query_grads.shape[0]) else mapped(plain)
        return run(query_grads, *others)

    return step
```
